32 devices in a mesh: rows: 2 (over y), cols: 16 (over z, x, core).
Axes of the slice: x: 2, y: 2, z: 4, core: 2. Of those that a mesh axis runs over, the one named last changes fastest.
Arguments:
- eigvecs: float32 [1024, 2048], P('rows', 'cols'), may hold values from -6 to 6
- wy_packed: float32 [32, 128, 128], P(('rows', 'cols')), may hold values from -6 to 6
- slot_block: int32 [2, 8, 2], P('rows'), may hold values from 0 to 1, each once within a row
Outputs:
- transformed: float32 [1024, 2048], P('rows', 'cols')
The draws below stay inside these ranges and needn't reach their ends.
Inputs may be any that keep to these rules, and one draw needn't show every extreme that they name: `slot_block`: for every group and level the 2 entries name each of 0 .. 1 once.
All inputs are finite; a program needn't handle non-finite values.
Results may differ from the reference program's by a relative error of at most 0.0003.
Values sent between devices are 32-bit elements; how exact they have to be, the bound alone decides.
A program may use at most 64 MiB of HBM per device.

```python
import jax
import jax.numpy as jnp
from jax import lax

BAND = 128
LEVELS = 8
HALF = 2
BLOCKS = 32
ROWS = 1024
COLS = 2048
N_ROWS = 2


def steps_of(own_key, dims, split, least, largest):
    loudness = 1.0
    for axis_at, parts in split:
        steps = jax.random.uniform(jax.random.fold_in(jax.random.fold_in(own_key, 6), axis_at), (parts,), jnp.float32, least / len(split), largest / len(split))
        loudness = loudness * jnp.repeat(jnp.exp(steps), dims[axis_at] // parts).reshape((-1,) + (1,) * (len(dims) - 1 - axis_at))
    return loudness


def normal_values(own_key, dims, spread, most, cuts=(), kind=jnp.bfloat16):
    values = jax.random.normal(own_key, dims, jnp.float32) * spread
    if len(cuts) > 0:
        values = steps_of(own_key, dims, cuts, -0.22, 0.18) * values
    return jnp.clip(values, min=-most, max=most).astype(kind)


def setup_inputs(seed: int = 0) -> dict:
    seeds = jax.random.split(jax.random.key(seed), 4)
    eigvecs = normal_values(seeds[0], (ROWS, COLS), 1.0, 6.0, ((0, 2), (1, 16)), jnp.float32)
    wy_packed = normal_values(seeds[1], (BLOCKS, BAND, BAND), 1.0, 6.0, ((0, 32),), jnp.float32)
    slot_block = jax.vmap(lambda own: jax.random.permutation(own, HALF))(jax.random.split(seeds[2], N_ROWS * LEVELS)).reshape((N_ROWS, LEVELS, HALF)).astype(jnp.int32)
    return dict(eigvecs=eigvecs, wy_packed=wy_packed, slot_block=slot_block)


highest = lax.Precision.HIGHEST


def unpack(packed):
    blocks, band_width = packed.shape[0], packed.shape[1]
    flipped = jnp.swapaxes(packed, 1, 2)
    padded = jnp.pad(flipped, ((0, 0), (0, 0), (0, band_width + 1)))
    flattened = padded.reshape(blocks, band_width * (2 * band_width + 1))[:, : 2 * band_width * band_width]
    return flattened.reshape(blocks, band_width, 2 * band_width)


def upper_inverse(upper):
    band_width = upper.shape[1]
    index_row = jnp.arange(band_width, dtype=jnp.int32)
    diag_values = jnp.diagonal(upper, axis1=1, axis2=2)
    identity = jnp.eye(band_width, dtype=upper.dtype)
    inverted = identity[None] * (1.0 / diag_values)[:, None, :]
    width = 1
    while width < band_width:
        same_new = (index_row[:, None] // (2 * width)) == (index_row[None, :] // (2 * width))
        same_old = (index_row[:, None] // width) == (index_row[None, :] // width)
        selector = jnp.logical_and(same_new, jnp.logical_not(same_old)).astype(upper.dtype)
        corner = upper * selector[None]
        partial_block = jnp.einsum("nij,njk->nik", corner, inverted, precision=highest)
        inverted = inverted - jnp.einsum("nij,njk->nik", inverted, partial_block, precision=highest)
        width = 2 * width
    return inverted


def wy_factor(reflectors):
    band_width = reflectors.shape[1]
    gram_matrix = jnp.einsum("njr,nkr->njk", reflectors, reflectors, precision=highest)
    identity = jnp.eye(band_width, dtype=gram_matrix.dtype)
    triangle = jnp.triu(gram_matrix, 1) + 0.5 * gram_matrix * identity
    return upper_inverse(triangle)


def reflect(reflectors, factors, windows):
    projected = jnp.einsum("njr,nrc->njc", reflectors, windows, precision=highest)
    scaled = jnp.einsum("njk,nkc->njc", factors, projected, precision=highest)
    return windows - jnp.einsum("njr,njc->nrc", reflectors, scaled, precision=highest)


def reference(eigvecs, wy_packed, slot_block):
    band_width = wy_packed.shape[1]
    row_count, col_count = eigvecs.shape
    groups = slot_block.shape[0]
    levels_all = slot_block.shape[1]
    per_level = slot_block.shape[2]
    unpacked = unpack(wy_packed)
    reflectors_all = unpacked.reshape(groups, levels_all, per_level, band_width, 2 * band_width)
    factors_all = wy_factor(unpacked).reshape(groups, levels_all, per_level, band_width, band_width)
    current = eigvecs
    padding = jnp.zeros((band_width, col_count), eigvecs.dtype)
    for level_index in range(levels_all):
        chosen = slot_block[:, level_index].astype(jnp.int32)[:, :, None, None]
        reflectors = jnp.take_along_axis(reflectors_all[:, level_index], chosen, axis=1)
        reflectors = reflectors.reshape(groups * per_level, band_width, 2 * band_width)
        factors = jnp.take_along_axis(factors_all[:, level_index], chosen, axis=1)
        factors = factors.reshape(groups * per_level, band_width, band_width)
        if level_index % 2 == 0:
            windows = current.reshape(groups * per_level, 2 * band_width, col_count)
            current = reflect(reflectors, factors, windows).reshape(row_count, col_count)
        else:
            extended = jnp.concatenate([current[band_width:], padding], axis=0)
            windows = extended.reshape(groups * per_level, 2 * band_width, col_count)
            result = reflect(reflectors, factors, windows).reshape(row_count, col_count)
            current = jnp.concatenate([current[:band_width], result[: row_count - band_width]], axis=0)
    return current
```

```python
import functools

import jax
import jax.numpy as jnp
from jax import lax
from jax.experimental import pallas as pl
from jax.experimental.pallas import tpu as pltpu
from jax.sharding import PartitionSpec as P

MESH = pl.DeviceIdType.MESH
F32 = jnp.float32
BF16 = jnp.bfloat16
NN = (((1,), (0,)), ((), ()))
NT = (((1,), (1,)), ((), ()))


def split(value):
    high = value.astype(BF16)
    low = (value - high.astype(F32)).astype(BF16)
    return high, low


def product(a, b, dims=NN):
    dot = functools.partial(lax.dot_general, dimension_numbers=dims, preferred_element_type=F32)
    return dot(a[0], b[0]) + (dot(a[0], b[1]) + dot(a[1], b[0]))


def exact(a, b, dims=NN):
    return lax.dot_general(
        a, b, dims, precision=lax.Precision.HIGHEST, preferred_element_type=F32
    )


def kernel(
    levels, n_rows, n_z, slot_ref, eig_ref, wy_ref, out_ref,
    wg, tg, xt, up_send, up_recv, down_send, down_recv,
    recv_sem, send_sem, own_sem, up_sem, down_sem,
):
    band = wy_ref.shape[1]
    chunks = eig_ref.shape[0] // band
    per_level = chunks // 2
    g = lax.axis_index("rows")
    c = lax.axis_index("cols")
    z, x, k = c // 4, (c // 2) % 2, c % 2
    x_partner = z * 4 + (1 - x) * 2 + k
    core_partner = z * 4 + x * 2 + (1 - k)
    z_mates = [((z + d) % n_z) * 4 + x * 2 + k for d in range(1, n_z)]
    has_above = g > 0
    has_below = g < n_rows - 1
    gathered = (wg, tg)

    barrier = pltpu.get_barrier_semaphore()
    for other in z_mates + [x_partner, core_partner]:
        pl.semaphore_signal(barrier, inc=1, device_id={"cols": other}, device_id_type=MESH)

    @pl.when(has_above)
    def _():
        pl.semaphore_signal(barrier, inc=1, device_id={"rows": g - 1}, device_id_type=MESH)

    @pl.when(has_below)
    def _():
        pl.semaphore_signal(barrier, inc=1, device_id={"rows": g + 1}, device_id_type=MESH)

    def block_copy(kind, block, target, sem):
        return pltpu.make_async_remote_copy(
            src_ref=gathered[kind].at[block],
            dst_ref=gathered[kind].at[block],
            send_sem=sem,
            recv_sem=recv_sem.at[kind, block],
            device_id={"cols": target},
            device_id_type=MESH,
        )

    def to_x(kind, zz, xx):
        return block_copy(kind, zz * 4 + xx * 2 + k, x_partner, send_sem.at[kind, zz * 2 + xx, 0])

    def to_core(kind, zz, xx):
        return block_copy(
            kind, zz * 4 + xx * 2 + k, core_partner, send_sem.at[kind, zz * 2 + xx, 1]
        )

    def to_z(kind, at):
        return block_copy(kind, c, z_mates[at], own_sem.at[kind, at])

    def send_own(kind):
        for at in range(n_z - 1):
            to_z(kind, at).start()
        to_x(kind, z, x).start()
        to_core(kind, z, x).start()

    def relay_z(kind, zz):
        @pl.when(z != zz)
        def _():
            to_x(kind, zz, x).wait_recv()
            to_x(kind, zz, x).start()
            to_core(kind, zz, x).start()

    def relay_x(kind, zz):
        to_core(kind, zz, 1 - x).wait_recv()
        to_core(kind, zz, 1 - x).start()

    sheared = pltpu.roll(jnp.transpose(wy_ref[0]), 0, 1, stride=1, stride_axis=0)
    wg[c] = sheared
    pl.semaphore_wait(
        barrier, n_z + 1 + has_above.astype(jnp.int32) + has_below.astype(jnp.int32)
    )
    send_own(0)

    for i in range(chunks):
        xt[i] = jnp.transpose(eig_ref[i * band : (i + 1) * band, :])

    row = lax.broadcasted_iota(jnp.int32, (band, band), 0)
    col = lax.broadcasted_iota(jnp.int32, (band, band), 1)
    upper = col >= row
    zero = jnp.zeros((band, band), F32)

    def spread(w):
        return jnp.concatenate([jnp.where(upper, w, zero), jnp.where(upper, zero, w)], axis=1)

    mine = spread(sheared)
    gram = exact(mine, mine, NT)
    diagonal = row == col
    on_diagonal = jnp.where(diagonal, 0.5 * gram, zero)
    by_row = 1.0 / jnp.sum(on_diagonal, axis=1, keepdims=True)
    by_col = 1.0 / jnp.sum(on_diagonal, axis=0, keepdims=True)
    strict = jnp.where(col > row, gram, zero)
    pairs = jnp.where(row // 2 == col // 2, strict, zero)
    inverse = jnp.where(diagonal, by_row, zero) - pairs * by_row * by_col
    width = 2
    while width < band:
        factor = 4 if width * 4 <= band else 2
        wide = width * factor
        inside = (row // wide == col // wide) & (row // width != col // width)
        corner = jnp.where(inside, strict, zero)
        nilpotent = exact(inverse, corner)
        stepped = inverse - exact(nilpotent, inverse)
        if factor == 4:
            stepped = stepped + exact(exact(nilpotent, nilpotent), stepped)
        inverse = stepped
        width = wide
        if width == 32:
            for zz in range(n_z):
                relay_z(0, zz)
    tg[c] = inverse
    send_own(1)
    for zz in range(n_z):
        relay_x(0, zz)
    for zz in range(n_z):
        relay_z(1, zz)

    def row_copy(src, dst, sem, at, target):
        return pltpu.make_async_remote_copy(
            src_ref=src.at[at],
            dst_ref=dst.at[at],
            send_sem=sem.at[0, at],
            recv_sem=sem.at[1, at],
            device_id={"rows": target},
            device_id_type=MESH,
        )

    def go_up(at):
        return row_copy(up_send, up_recv, up_sem, at, g - 1)

    def go_down(at):
        return row_copy(down_send, down_recv, down_sem, at, g + 1)

    def reflected(operators, top, bottom):
        z_parts, v_parts = operators
        pair = jnp.concatenate([top, bottom], axis=1)
        projected = product(split(pair), z_parts, NT)
        return pair - product(split(projected), v_parts)

    for level in range(levels):
        zz, xx = level // 2, level % 2
        for kind in range(2):
            other = 4 * zz + 2 * xx + 1 - k
            if kind == 1:
                @pl.when(x != xx)
                def _():
                    relay_x(1, zz)
            block_copy(kind, other, core_partner, send_sem.at[0, 0, 0]).wait_recv()
        stored = [(wg[level * per_level + s], tg[level * per_level + s]) for s in range(per_level)]
        operators = []
        for h in range(per_level):
            first = slot_ref[0, level, h] == 0
            w = jnp.where(first, stored[0][0], stored[1][0])
            t = jnp.where(first, stored[0][1], stored[1][1])
            v_parts = split(spread(w))
            z_parts = split(product(split(t), v_parts))
            operators.append((z_parts, v_parts))
        if level % 2 == 0:
            for h in range(per_level):
                new = reflected(operators[h], xt[2 * h], xt[2 * h + 1])
                xt[2 * h] = new[:, :band]
                xt[2 * h + 1] = new[:, band:]
        else:
            at = level // 2

            @pl.when(has_above)
            def _():
                up_send[at] = xt[0]
                go_up(at).start()

            for h in range(per_level - 1):
                new = reflected(operators[h], xt[2 * h + 1], xt[2 * h + 2])
                xt[2 * h + 1] = new[:, :band]
                xt[2 * h + 2] = new[:, band:]

            @pl.when(has_below)
            def _():
                go_up(at).wait_recv()

            @pl.when(jnp.logical_not(has_below))
            def _():
                up_recv[at] = zero

            new = reflected(operators[per_level - 1], xt[chunks - 1], up_recv[at])
            xt[chunks - 1] = new[:, :band]

            @pl.when(has_below)
            def _():
                down_send[at] = new[:, band:]
                go_down(at).start()

            @pl.when(has_above)
            def _():
                go_down(at).wait_recv()
                xt[0] = down_recv[at]

    for i in range(chunks):
        out_ref[i * band : (i + 1) * band, :] = jnp.transpose(xt[i])

    for kind in range(2):
        for at in range(n_z - 1):
            to_z(kind, at).wait_send()
        for zz in range(n_z):
            to_x(kind, zz, x).wait_send()
            for xx in range(2):
                to_core(kind, zz, xx).wait_send()
    for at in range(levels // 2):
        @pl.when(has_above)
        def _():
            go_up(at).wait_send()

        @pl.when(has_below)
        def _():
            go_down(at).wait_send()


def per_device(n_rows, n_cols, eigvecs, wy_packed, slot_block):
    band = wy_packed.shape[1]
    levels, per_level = slot_block.shape[1:]
    n_z = n_cols // 4
    assert n_cols == levels * per_level and n_cols % 4 == 0
    assert wy_packed.shape[0] == 1 and per_level == 2
    tile = (band, eigvecs.shape[1])
    blocks = pltpu.VMEM((n_cols, band, band), F32)
    slots = pltpu.VMEM((levels // 2,) + tile, F32)
    vmem = pl.BlockSpec(memory_space=pltpu.VMEM)
    return pl.pallas_call(
        functools.partial(kernel, levels, n_rows, n_z),
        out_shape=jax.ShapeDtypeStruct(eigvecs.shape, F32),
        in_specs=[pl.BlockSpec(memory_space=pltpu.SMEM), vmem, vmem],
        out_specs=vmem,
        scratch_shapes=[
            blocks,
            blocks,
            pltpu.VMEM((eigvecs.shape[0] // band,) + tile, F32),
            slots,
            slots,
            slots,
            slots,
            pltpu.SemaphoreType.DMA((2, n_cols)),
            pltpu.SemaphoreType.DMA((2, n_cols // 2, 2)),
            pltpu.SemaphoreType.DMA((2, n_z - 1)),
            pltpu.SemaphoreType.DMA((2, levels // 2)),
            pltpu.SemaphoreType.DMA((2, levels // 2)),
        ],
        compiler_params=pltpu.CompilerParams(collective_id=0, has_side_effects=True),
    )(slot_block, eigvecs, wy_packed)


def solution(mesh):
    placed = (P("rows", "cols"), P(("rows", "cols"), None, None), P("rows", None, None))
    return jax.shard_map(
        functools.partial(per_device, mesh.shape["rows"], mesh.shape["cols"]),
        mesh=mesh, in_specs=placed, out_specs=P("rows", "cols"), check_vma=False,
    )
```

```python
import functools

import jax
import jax.numpy as jnp
from jax import lax
from jax.experimental import pallas as pl
from jax.experimental.pallas import tpu as pltpu
from jax.sharding import PartitionSpec as P

MESH = pl.DeviceIdType.MESH
F32 = jnp.float32
BF16 = jnp.bfloat16
NN = (((1,), (0,)), ((), ()))
NT = (((1,), (1,)), ((), ()))


def split(value):
    high = value.astype(BF16)
    low = (value - high.astype(F32)).astype(BF16)
    return high, low


def product(a, b, dims=NN):
    dot = functools.partial(lax.dot_general, dimension_numbers=dims, preferred_element_type=F32)
    return dot(a[0], b[0]) + (dot(a[0], b[1]) + dot(a[1], b[0]))


def inverses(grams, multiply):
    band = grams[0].shape[0]
    row = lax.broadcasted_iota(jnp.int32, (band, band), 0)
    col = lax.broadcasted_iota(jnp.int32, (band, band), 1)
    zero = jnp.zeros((band, band), F32)
    diagonal = row == col
    stricts, found = [], []
    for gram in grams:
        on_diagonal = jnp.where(diagonal, 0.5 * gram, zero)
        by_row = 1.0 / jnp.sum(on_diagonal, axis=1, keepdims=True)
        by_col = 1.0 / jnp.sum(on_diagonal, axis=0, keepdims=True)
        strict = jnp.where(col > row, gram, zero)
        pairs = jnp.where(row // 2 == col // 2, strict, zero)
        stricts.append(strict)
        found.append(jnp.where(diagonal, by_row, zero) - pairs * by_row * by_col)
    width = 2
    while width < band:
        factor = 4 if width * 4 <= band else 2
        wide = width * factor
        inside = (row // wide == col // wide) & (row // width != col // width)
        corners = [jnp.where(inside, strict, zero) for strict in stricts]
        powers = [multiply(a, b) for a, b in zip(found, corners)]
        firsts = [multiply(n, a) for n, a in zip(powers, found)]
        found = [a - b for a, b in zip(found, firsts)]
        if factor == 4:
            squares = [multiply(n, n) for n in powers]
            seconds = [multiply(n, a) for n, a in zip(squares, found)]
            found = [a + b for a, b in zip(found, seconds)]
        width = wide
    return found


def fast(a, b):
    return product(split(a), split(b))


def kernel(
    levels, n_rows, n_z, slot_ref, eig_ref, wy_ref, out_ref,
    wg, xt, ops, half_send, above, up_send, up_recv, down_send, down_recv,
    recv_sem, send_sem, own_sem, up_sem, down_sem, half_sem, side_sem,
):
    band = wy_ref.shape[1]
    chunks = eig_ref.shape[0] // band
    per_level = chunks // 2
    rounds = levels // 2
    g = lax.axis_index("rows")
    c = lax.axis_index("cols")
    z, x, k = c // 4, (c // 2) % 2, c % 2
    x_partner = z * 4 + (1 - x) * 2 + k
    core_partner = z * 4 + x * 2 + (1 - k)
    z_mates = [((z + d) % n_z) * 4 + x * 2 + k for d in range(1, n_z)]
    has_above = g > 0
    has_below = g < n_rows - 1

    barrier = pltpu.get_barrier_semaphore()
    for other in z_mates + [x_partner, core_partner]:
        pl.semaphore_signal(barrier, inc=1, device_id={"cols": other}, device_id_type=MESH)

    @pl.when(has_above)
    def _():
        pl.semaphore_signal(barrier, inc=1, device_id={"rows": g - 1}, device_id_type=MESH)

    @pl.when(has_below)
    def _():
        pl.semaphore_signal(barrier, inc=1, device_id={"rows": g + 1}, device_id_type=MESH)

    def block_copy(block, target, sem):
        return pltpu.make_async_remote_copy(
            src_ref=wg.at[block],
            dst_ref=wg.at[block],
            send_sem=sem,
            recv_sem=recv_sem.at[block],
            device_id={"cols": target},
            device_id_type=MESH,
        )

    def to_x(zz, xx):
        return block_copy(zz * 4 + xx * 2 + k, x_partner, send_sem.at[zz * 2 + xx, 0])

    def to_core(zz, xx):
        return block_copy(zz * 4 + xx * 2 + k, core_partner, send_sem.at[zz * 2 + xx, 1])

    def to_z(at):
        return block_copy(c, z_mates[at], own_sem.at[at])

    def relay_x(zz):
        to_core(zz, 1 - x).wait_recv()
        to_core(zz, 1 - x).start()

    def wait_core(zz):
        for xx in range(2):
            block_copy(zz * 4 + xx * 2 + 1 - k, core_partner, send_sem.at[0, 0]).wait_recv()

    def row_copy(src, dst, sem, at, target):
        return pltpu.make_async_remote_copy(
            src_ref=src.at[at],
            dst_ref=dst.at[at],
            send_sem=sem.at[0, at],
            recv_sem=sem.at[1, at],
            device_id={"rows": target},
            device_id_type=MESH,
        )

    def go_up(at):
        return row_copy(up_send, up_recv, up_sem, at, g - 1)

    def go_down(at):
        return row_copy(down_send, down_recv, down_sem, at, g + 1)

    half = band // 2

    def half_down(at):
        return pltpu.make_async_remote_copy(
            src_ref=half_send.at[at],
            dst_ref=above.at[at, pl.ds(k * half, half)],
            send_sem=half_sem.at[0, at],
            recv_sem=half_sem.at[1, at],
            device_id={"rows": g + 1},
            device_id_type=MESH,
        )

    def half_side(at):
        return pltpu.make_async_remote_copy(
            src_ref=above.at[at, pl.ds(k * half, half)],
            dst_ref=above.at[at, pl.ds(k * half, half)],
            send_sem=side_sem.at[0, at],
            recv_sem=side_sem.at[1, at],
            device_id={"cols": core_partner},
            device_id_type=MESH,
        )

    def send_half(at):
        level = 2 * at + 1
        first = slot_ref[0, level, per_level - 1] == 0
        rows = pl.ds(k * half, half)
        half_send[at] = jnp.where(
            first, wg[level * per_level, rows], wg[level * per_level + 1, rows]
        )
        half_down(at).start()

    wg[c] = pltpu.roll(jnp.transpose(wy_ref[0]), 0, 1, stride=1, stride_axis=0)
    pl.semaphore_wait(
        barrier, n_z + 1 + has_above.astype(jnp.int32) + has_below.astype(jnp.int32)
    )
    for at in range(n_z - 1):
        to_z(at).start()
    to_x(z, x).start()
    to_core(z, x).start()

    @pl.when(jnp.logical_not(has_above))
    def _():
        above[...] = jnp.zeros_like(above)
        down_recv[...] = jnp.zeros_like(down_recv)

    @pl.when(jnp.logical_not(has_below))
    def _():
        up_recv[...] = jnp.zeros_like(up_recv)

    for i in range(chunks):
        xt[i] = jnp.transpose(eig_ref[i * band : (i + 1) * band, :])

    row = lax.broadcasted_iota(jnp.int32, (band, band), 0)
    col = lax.broadcasted_iota(jnp.int32, (band, band), 1)
    upper = col >= row
    zero = jnp.zeros((band, band), F32)

    def spread(w):
        return jnp.concatenate([jnp.where(upper, w, zero), jnp.where(upper, zero, w)], axis=1)

    def chosen(level, h):
        first = slot_ref[0, level, h] == 0
        return jnp.where(first, wg[level * per_level], wg[level * per_level + 1])

    def prepare(sheared, places):
        v_parts = [split(spread(w)) for w in sheared]
        grams = [product(v, v, NT) for v in v_parts]
        factors = inverses(grams, fast)
        for place, v, t in zip(places, v_parts, factors):
            z_parts = split(product(split(t), v))
            ops[place, 0] = z_parts[0]
            ops[place, 1] = z_parts[1]
            ops[place, 2] = v[0]
            ops[place, 3] = v[1]

    def reflected(place, top, bottom):
        pair = jnp.concatenate([top, bottom], axis=1)
        projected = product(split(pair), (ops[place, 0], ops[place, 1]), NT)
        new = pair - product(split(projected), (ops[place, 2], ops[place, 3]))
        return new[:, :band], new[:, band:]

    for zz in range(n_z):
        @pl.when(z != zz)
        def _():
            to_x(zz, x).wait_recv()
            to_x(zz, x).start()
            to_core(zz, x).start()

    relay_x(0)
    wait_core(0)

    @pl.when(has_below)
    def _():
        send_half(0)

    prepare([chosen(0, 0), chosen(0, 1)], [3, 4])

    def both_levels(at, carry):
        for h in range(per_level):
            xt[2 * h], xt[2 * h + 1] = reflected(3 + h, xt[2 * h], xt[2 * h + 1])

        @pl.when(has_above)
        def _():
            up_send[at] = xt[0]
            go_up(at).start()

        @pl.when(has_below)
        def _():
            down_send[at] = xt[chunks - 1]
            go_down(at).start()

        @pl.when(at < rounds - 1)
        def _():
            relay_x(at + 1)
            wait_core(at + 1)

            @pl.when(has_below)
            def _():
                send_half(at + 1)

        @pl.when(has_above)
        def _():
            half_down(at).wait_recv()
            half_side(at).start()
            half_side(at).wait_recv()

        odd, even = 2 * at + 1, (2 * at + 2) % levels
        prepare(
            [chosen(odd, 0), chosen(odd, 1), above[at], chosen(even, 0), chosen(even, 1)],
            [0, 1, 2, 3, 4],
        )
        xt[1], xt[2] = reflected(0, xt[1], xt[2])

        @pl.when(has_below)
        def _():
            go_up(at).wait_recv()

        @pl.when(has_above)
        def _():
            go_down(at).wait_recv()

        last, _ = reflected(1, xt[chunks - 1], up_recv[at])
        _, first = reflected(2, down_recv[at], xt[0])
        xt[chunks - 1] = last
        xt[0] = jnp.where(has_above, first, xt[0])
        return carry

    lax.fori_loop(0, rounds, both_levels, 0)

    for i in range(chunks):
        out_ref[i * band : (i + 1) * band, :] = jnp.transpose(xt[i])

    for at in range(n_z - 1):
        to_z(at).wait_send()
    for zz in range(n_z):
        to_x(zz, x).wait_send()
        for xx in range(2):
            to_core(zz, xx).wait_send()
    for at in range(rounds):
        @pl.when(has_above)
        def _():
            go_up(at).wait_send()
            half_side(at).wait_send()

        @pl.when(has_below)
        def _():
            go_down(at).wait_send()
            half_down(at).wait_send()


def per_device(n_rows, n_cols, eigvecs, wy_packed, slot_block):
    band = wy_packed.shape[1]
    rows, cols = eigvecs.shape
    levels, per_level = slot_block.shape[1:]
    n_z = n_cols // 4
    rounds = levels // 2
    assert n_cols == levels * per_level and n_z == rounds
    assert wy_packed.shape[0] == 1 and per_level == 2 and rows == 4 * band
    blocks = pltpu.VMEM((rounds, band, band), F32)
    slots = pltpu.VMEM((rounds, cols, band), F32)
    vmem = pl.BlockSpec(memory_space=pltpu.VMEM)
    in_order = pltpu.SemaphoreType.DMA((2, rounds))
    return pl.pallas_call(
        functools.partial(kernel, levels, n_rows, n_z),
        out_shape=jax.ShapeDtypeStruct(eigvecs.shape, F32),
        in_specs=[pl.BlockSpec(memory_space=pltpu.SMEM), vmem, vmem],
        out_specs=vmem,
        scratch_shapes=[
            pltpu.VMEM((n_cols, band, band), F32),
            pltpu.VMEM((rows // band, cols, band), F32),
            pltpu.VMEM((5, 4, band, 2 * band), BF16),
            pltpu.VMEM((rounds, band // 2, band), F32),
            blocks,
            slots,
            slots,
            slots,
            slots,
            pltpu.SemaphoreType.DMA((n_cols,)),
            pltpu.SemaphoreType.DMA((n_cols // 2, 2)),
            pltpu.SemaphoreType.DMA((n_z - 1,)),
            in_order,
            in_order,
            in_order,
            in_order,
        ],
        compiler_params=pltpu.CompilerParams(collective_id=0, has_side_effects=True),
    )(slot_block, eigvecs, wy_packed)


def solution(mesh):
    placed = (P("rows", "cols"), P(("rows", "cols"), None, None), P("rows", None, None))
    return jax.shard_map(
        functools.partial(per_device, mesh.shape["rows"], mesh.shape["cols"]),
        mesh=mesh, in_specs=placed, out_specs=P("rows", "cols"), check_vma=False,
    )
```

```python
import functools

import jax
import jax.numpy as jnp
from jax import lax
from jax.experimental import pallas as pl
from jax.experimental.pallas import tpu as pltpu
from jax.sharding import PartitionSpec as P

MESH = pl.DeviceIdType.MESH
F32 = jnp.float32
BF16 = jnp.bfloat16
NN = (((1,), (0,)), ((), ()))
NT = (((1,), (1,)), ((), ()))


def split(value):
    high = value.astype(BF16)
    low = (value - high.astype(F32)).astype(BF16)
    return high, low


def product(a, b, dims=NN):
    dot = functools.partial(lax.dot_general, dimension_numbers=dims, preferred_element_type=F32)
    return dot(a[0], b[0]) + (dot(a[0], b[1]) + dot(a[1], b[0]))


def inverses(grams, multiply):
    band = grams[0].shape[0]
    row = lax.broadcasted_iota(jnp.int32, (band, band), 0)
    col = lax.broadcasted_iota(jnp.int32, (band, band), 1)
    zero = jnp.zeros((band, band), F32)
    diagonal = row == col
    stricts, found = [], []
    for gram in grams:
        on_diagonal = jnp.where(diagonal, 0.5 * gram, zero)
        by_row = 1.0 / jnp.sum(on_diagonal, axis=1, keepdims=True)
        by_col = 1.0 / jnp.sum(on_diagonal, axis=0, keepdims=True)
        strict = jnp.where(col > row, gram, zero)
        pairs = jnp.where(row // 2 == col // 2, strict, zero)
        stricts.append(strict)
        found.append(jnp.where(diagonal, by_row, zero) - pairs * by_row * by_col)
    width = 2
    while width < band:
        factor = 4 if width * 4 <= band else 2
        wide = width * factor
        inside = (row // wide == col // wide) & (row // width != col // width)
        corners = [jnp.where(inside, strict, zero) for strict in stricts]
        powers = [multiply(a, b) for a, b in zip(found, corners)]
        firsts = [multiply(n, a) for n, a in zip(powers, found)]
        found = [a - b for a, b in zip(found, firsts)]
        if factor == 4:
            squares = [multiply(n, n) for n in powers]
            seconds = [multiply(n, a) for n, a in zip(squares, found)]
            found = [a + b for a, b in zip(found, seconds)]
        width = wide
    return found


def fast(a, b):
    return product(split(a), split(b))


def kernel(
    levels, n_rows, n_z, slot_ref, eig_ref, wy_ref, out_ref,
    wg, xt, ops, half_send, above, up_send, up_recv, down_send, down_recv,
    recv_sem, send_sem, own_sem, up_sem, down_sem, half_sem, side_sem,
):
    band = wy_ref.shape[1]
    chunks = eig_ref.shape[0] // band
    per_level = chunks // 2
    rounds = levels // 2
    g = lax.axis_index("rows")
    c = lax.axis_index("cols")
    z, x, k = c // 4, (c // 2) % 2, c % 2
    x_partner = z * 4 + (1 - x) * 2 + k
    core_partner = z * 4 + x * 2 + (1 - k)
    z_mates = [((z + d) % n_z) * 4 + x * 2 + k for d in range(1, n_z)]
    has_above = g > 0
    has_below = g < n_rows - 1

    barrier = pltpu.get_barrier_semaphore()
    for other in z_mates + [x_partner, core_partner]:
        pl.semaphore_signal(barrier, inc=1, device_id={"cols": other}, device_id_type=MESH)

    @pl.when(has_above)
    def _():
        pl.semaphore_signal(barrier, inc=1, device_id={"rows": g - 1}, device_id_type=MESH)

    @pl.when(has_below)
    def _():
        pl.semaphore_signal(barrier, inc=1, device_id={"rows": g + 1}, device_id_type=MESH)

    def block_copy(block, target, sem):
        return pltpu.make_async_remote_copy(
            src_ref=wg.at[block],
            dst_ref=wg.at[block],
            send_sem=sem,
            recv_sem=recv_sem.at[block],
            device_id={"cols": target},
            device_id_type=MESH,
        )

    def to_x(zz, xx):
        return block_copy(zz * 4 + xx * 2 + k, x_partner, send_sem.at[zz * 2 + xx, 0])

    def to_core(zz, xx):
        return block_copy(zz * 4 + xx * 2 + k, core_partner, send_sem.at[zz * 2 + xx, 1])

    def to_z(zz):
        return block_copy(c, zz * 4 + x * 2 + k, own_sem.at[zz])

    def relay_z(zz):
        @pl.when(z != zz)
        def _():
            to_x(zz, x).wait_recv()
            to_x(zz, x).start()
            to_core(zz, x).start()

    def relay_x(zz):
        to_core(zz, 1 - x).wait_recv()
        to_core(zz, 1 - x).start()

    def wait_core(zz):
        for xx in range(2):
            block_copy(zz * 4 + xx * 2 + 1 - k, core_partner, send_sem.at[0, 0]).wait_recv()

    def row_copy(src, dst, sem, at, target):
        return pltpu.make_async_remote_copy(
            src_ref=src.at[at],
            dst_ref=dst.at[at],
            send_sem=sem.at[0, at],
            recv_sem=sem.at[1, at],
            device_id={"rows": target},
            device_id_type=MESH,
        )

    def go_up(at):
        return row_copy(up_send, up_recv, up_sem, at, g - 1)

    def go_down(at):
        return row_copy(down_send, down_recv, down_sem, at, g + 1)

    half = band // 2

    def half_down(at):
        return pltpu.make_async_remote_copy(
            src_ref=half_send.at[at],
            dst_ref=above.at[at, pl.ds(k * half, half)],
            send_sem=half_sem.at[0, at],
            recv_sem=half_sem.at[1, at],
            device_id={"rows": g + 1},
            device_id_type=MESH,
        )

    def half_side(at):
        return pltpu.make_async_remote_copy(
            src_ref=above.at[at, pl.ds(k * half, half)],
            dst_ref=above.at[at, pl.ds(k * half, half)],
            send_sem=side_sem.at[0, at],
            recv_sem=side_sem.at[1, at],
            device_id={"cols": core_partner},
            device_id_type=MESH,
        )

    def send_half(at):
        level = 2 * at + 1
        first = slot_ref[0, per_level - 1, level] == 0
        rows = pl.ds(k * half, half)
        half_send[at] = jnp.where(
            first, wg[level * per_level, rows], wg[level * per_level + 1, rows]
        )
        half_down(at).start()

    wg[c] = pltpu.roll(jnp.transpose(wy_ref[0]), 0, 1, stride=1, stride_axis=0)
    pl.semaphore_wait(
        barrier, n_z + 1 + has_above.astype(jnp.int32) + has_below.astype(jnp.int32)
    )
    to_x(z, x).start()
    to_core(z, x).start()
    for far in range(n_z - 1, -1, -1):
        @pl.when((far != z) & ((far < z) | (z < 2)))
        def _():
            to_z(far).start()

    @pl.when(jnp.logical_not(has_above))
    def _():
        above[...] = jnp.zeros_like(above)
        down_recv[...] = jnp.zeros_like(down_recv)

    @pl.when(jnp.logical_not(has_below))
    def _():
        up_recv[...] = jnp.zeros_like(up_recv)

    for i in range(chunks):
        xt[i] = jnp.transpose(eig_ref[i * band : (i + 1) * band, :])

    row = lax.broadcasted_iota(jnp.int32, (band, band), 0)
    col = lax.broadcasted_iota(jnp.int32, (band, band), 1)
    upper = col >= row
    zero = jnp.zeros((band, band), F32)

    def spread(w):
        return jnp.concatenate([jnp.where(upper, w, zero), jnp.where(upper, zero, w)], axis=1)

    def chosen(level, h):
        first = slot_ref[0, h, level] == 0
        return jnp.where(first, wg[level * per_level], wg[level * per_level + 1])

    def prepare(sheared, places):
        v_parts = [split(spread(w)) for w in sheared]
        grams = [product(v, v, NT) for v in v_parts]
        factors = inverses(grams, fast)
        for place, v, t in zip(places, v_parts, factors):
            z_parts = split(product(split(t), v))
            ops[place, 0] = z_parts[0]
            ops[place, 1] = z_parts[1]
            ops[place, 2] = v[0]
            ops[place, 3] = v[1]

    def reflected(place, top, bottom):
        pair = jnp.concatenate([top, bottom], axis=1)
        projected = product(split(pair), (ops[place, 0], ops[place, 1]), NT)
        new = pair - product(split(projected), (ops[place, 2], ops[place, 3]))
        return new[:, :band], new[:, band:]

    relay_z(0)

    @pl.when(z >= 2)
    def _():
        for far in range(n_z - 1, 2, -1):
            @pl.when(far > z)
            def _():
                to_z(far).start()

    relay_x(0)
    wait_core(0)

    @pl.when(has_below)
    def _():
        send_half(0)

    relay_z(1)
    prepare([chosen(0, 0), chosen(0, 1)], [3, 4])

    def both_levels(at, carry):
        @pl.when(has_above)
        def _():
            half_down(at).wait_recv()
            half_side(at).start()

        for h in range(per_level):
            xt[2 * h], xt[2 * h + 1] = reflected(3 + h, xt[2 * h], xt[2 * h + 1])

        @pl.when(has_above)
        def _():
            up_send[at] = xt[0]
            go_up(at).start()

        @pl.when(has_below)
        def _():
            down_send[at] = xt[chunks - 1]
            go_down(at).start()

        @pl.when(at < rounds - 1)
        def _():
            relay_x(at + 1)
            wait_core(at + 1)

            @pl.when(has_below)
            def _():
                send_half(at + 1)

        @pl.when(at < rounds - 2)
        def _():
            relay_z(at + 2)

        @pl.when(has_above)
        def _():
            half_side(at).wait_recv()

        odd, even = 2 * at + 1, (2 * at + 2) % levels
        prepare(
            [chosen(odd, 0), chosen(odd, 1), above[at], chosen(even, 0), chosen(even, 1)],
            [0, 1, 2, 3, 4],
        )
        xt[1], xt[2] = reflected(0, xt[1], xt[2])

        @pl.when(has_below)
        def _():
            go_up(at).wait_recv()

        @pl.when(has_above)
        def _():
            go_down(at).wait_recv()

        last, _ = reflected(1, xt[chunks - 1], up_recv[at])
        _, first = reflected(2, down_recv[at], xt[0])
        xt[chunks - 1] = last
        xt[0] = jnp.where(has_above, first, xt[0])
        return carry

    lax.fori_loop(0, rounds, both_levels, 0)

    for i in range(chunks):
        out_ref[i * band : (i + 1) * band, :] = jnp.transpose(xt[i])

    for zz in range(n_z):
        @pl.when(z != zz)
        def _():
            to_z(zz).wait_send()

    for zz in range(n_z):
        to_x(zz, x).wait_send()
        for xx in range(2):
            to_core(zz, xx).wait_send()
    for at in range(rounds):
        @pl.when(has_above)
        def _():
            go_up(at).wait_send()
            half_side(at).wait_send()

        @pl.when(has_below)
        def _():
            go_down(at).wait_send()
            half_down(at).wait_send()


def per_device(n_rows, n_cols, eigvecs, wy_packed, slot_block):
    band = wy_packed.shape[1]
    rows, cols = eigvecs.shape
    levels, per_level = slot_block.shape[1:]
    n_z = n_cols // 4
    rounds = levels // 2
    assert n_cols == levels * per_level and n_z == rounds
    assert wy_packed.shape[0] == 1 and per_level == 2 and rows == 4 * band
    blocks = pltpu.VMEM((rounds, band, band), F32)
    slots = pltpu.VMEM((rounds, cols, band), F32)
    vmem = pl.BlockSpec(memory_space=pltpu.VMEM)
    in_order = pltpu.SemaphoreType.DMA((2, rounds))
    return pl.pallas_call(
        functools.partial(kernel, levels, n_rows, n_z),
        out_shape=jax.ShapeDtypeStruct(eigvecs.shape, F32),
        in_specs=[pl.BlockSpec(memory_space=pltpu.SMEM), vmem, vmem],
        out_specs=vmem,
        scratch_shapes=[
            pltpu.VMEM((n_cols, band, band), F32),
            pltpu.VMEM((rows // band, cols, band), F32),
            pltpu.VMEM((5, 4, band, 2 * band), BF16),
            pltpu.VMEM((rounds, band // 2, band), F32),
            blocks,
            slots,
            slots,
            slots,
            slots,
            pltpu.SemaphoreType.DMA((n_cols,)),
            pltpu.SemaphoreType.DMA((n_cols // 2, 2)),
            pltpu.SemaphoreType.DMA((n_z,)),
            in_order,
            in_order,
            in_order,
            in_order,
        ],
        compiler_params=pltpu.CompilerParams(collective_id=0, has_side_effects=True),
    )(jnp.swapaxes(slot_block, 1, 2), eigvecs, wy_packed)


def solution(mesh):
    placed = (P("rows", "cols"), P(("rows", "cols"), None, None), P("rows", None, None))
    return jax.shard_map(
        functools.partial(per_device, mesh.shape["rows"], mesh.shape["cols"]),
        mesh=mesh, in_specs=placed, out_specs=P("rows", "cols"), check_vma=False,
    )
```

```python
import functools

import jax
import jax.numpy as jnp
from jax import lax
from jax.experimental import pallas as pl
from jax.experimental.pallas import tpu as pltpu
from jax.sharding import PartitionSpec as P

MESH = pl.DeviceIdType.MESH
F32 = jnp.float32
BF16 = jnp.bfloat16
NN = (((1,), (0,)), ((), ()))
NT = (((1,), (1,)), ((), ()))


def split(value):
    high = value.astype(BF16)
    low = (value - high.astype(F32)).astype(BF16)
    return high, low


def product(a, b, dims=NN):
    dot = functools.partial(lax.dot_general, dimension_numbers=dims, preferred_element_type=F32)
    return dot(a[0], b[0]) + (dot(a[0], b[1]) + dot(a[1], b[0]))


def inverses(grams, multiply):
    band = grams[0].shape[0]
    row = lax.broadcasted_iota(jnp.int32, (band, band), 0)
    col = lax.broadcasted_iota(jnp.int32, (band, band), 1)
    zero = jnp.zeros((band, band), F32)
    diagonal = row == col
    stricts, found = [], []
    for gram in grams:
        on_diagonal = jnp.where(diagonal, 0.5 * gram, zero)
        by_row = 1.0 / jnp.sum(on_diagonal, axis=1, keepdims=True)
        by_col = 1.0 / jnp.sum(on_diagonal, axis=0, keepdims=True)
        strict = jnp.where(col > row, gram, zero)
        pairs = jnp.where(row // 2 == col // 2, strict, zero)
        stricts.append(strict)
        found.append(jnp.where(diagonal, by_row, zero) - pairs * by_row * by_col)
    width = 2
    while width < band:
        factor = 4 if width * 4 <= band else 2
        wide = width * factor
        inside = (row // wide == col // wide) & (row // width != col // width)
        corners = [jnp.where(inside, strict, zero) for strict in stricts]
        powers = [multiply(a, b) for a, b in zip(found, corners)]
        firsts = [multiply(n, a) for n, a in zip(powers, found)]
        found = [a - b for a, b in zip(found, firsts)]
        if factor == 4:
            squares = [multiply(n, n) for n in powers]
            seconds = [multiply(n, a) for n, a in zip(squares, found)]
            found = [a + b for a, b in zip(found, seconds)]
        width = wide
    return found


def fast(a, b):
    return product(split(a), split(b))


def kernel(
    levels, n_rows, n_z, slot_ref, eig_ref, wy_ref, out_ref,
    wg, xt, ops, half_send, above, up_send, up_recv, down_send, down_recv,
    recv_sem, send_sem, own_sem, up_sem, down_sem, half_sem, side_sem,
):
    band = wy_ref.shape[1]
    chunks = eig_ref.shape[0] // band
    per_level = chunks // 2
    rounds = levels // 2
    g = lax.axis_index("rows")
    c = lax.axis_index("cols")
    z, x, k = c // 4, (c // 2) % 2, c % 2
    x_partner = z * 4 + (1 - x) * 2 + k
    core_partner = z * 4 + x * 2 + (1 - k)
    z_mates = [((z + d) % n_z) * 4 + x * 2 + k for d in range(1, n_z)]
    has_above = g > 0
    has_below = g < n_rows - 1

    barrier = pltpu.get_barrier_semaphore()
    for other in z_mates + [x_partner, core_partner]:
        pl.semaphore_signal(barrier, inc=1, device_id={"cols": other}, device_id_type=MESH)

    @pl.when(has_above)
    def _():
        pl.semaphore_signal(barrier, inc=1, device_id={"rows": g - 1}, device_id_type=MESH)

    @pl.when(has_below)
    def _():
        pl.semaphore_signal(barrier, inc=1, device_id={"rows": g + 1}, device_id_type=MESH)

    def block_copy(block, target, sem):
        return pltpu.make_async_remote_copy(
            src_ref=wg.at[block],
            dst_ref=wg.at[block],
            send_sem=sem,
            recv_sem=recv_sem.at[block],
            device_id={"cols": target},
            device_id_type=MESH,
        )

    def to_x(zz, xx):
        return block_copy(zz * 4 + xx * 2 + k, x_partner, send_sem.at[zz * 2 + xx, 0])

    def to_core(zz, xx):
        return block_copy(zz * 4 + xx * 2 + k, core_partner, send_sem.at[zz * 2 + xx, 1])

    def to_z(zz):
        return block_copy(c, zz * 4 + x * 2 + k, own_sem.at[zz])

    def relay_z(zz):
        @pl.when(z != zz)
        def _():
            to_x(zz, x).wait_recv()
            to_x(zz, x).start()
            to_core(zz, x).start()

    def relay_x(zz):
        to_core(zz, 1 - x).wait_recv()
        to_core(zz, 1 - x).start()

    def wait_core(zz):
        for xx in range(2):
            block_copy(zz * 4 + xx * 2 + 1 - k, core_partner, send_sem.at[0, 0]).wait_recv()

    def row_copy(src, dst, sem, at, target):
        return pltpu.make_async_remote_copy(
            src_ref=src.at[at],
            dst_ref=dst.at[at],
            send_sem=sem.at[0, at],
            recv_sem=sem.at[1, at],
            device_id={"rows": target},
            device_id_type=MESH,
        )

    def go_up(at):
        return row_copy(up_send, up_recv, up_sem, at, g - 1)

    def go_down(at):
        return row_copy(down_send, down_recv, down_sem, at, g + 1)

    half = band // 2

    def half_down(at):
        return pltpu.make_async_remote_copy(
            src_ref=half_send.at[at],
            dst_ref=above.at[at, pl.ds(k * half, half)],
            send_sem=half_sem.at[0, at],
            recv_sem=half_sem.at[1, at],
            device_id={"rows": g + 1},
            device_id_type=MESH,
        )

    def half_side(at):
        return pltpu.make_async_remote_copy(
            src_ref=above.at[at, pl.ds(k * half, half)],
            dst_ref=above.at[at, pl.ds(k * half, half)],
            send_sem=side_sem.at[0, at],
            recv_sem=side_sem.at[1, at],
            device_id={"cols": core_partner},
            device_id_type=MESH,
        )

    def send_half(at):
        level = 2 * at + 1
        first = slot_ref[0, per_level - 1, level] == 0
        rows = pl.ds(k * half, half)
        half_send[at] = jnp.where(
            first, wg[level * per_level, rows], wg[level * per_level + 1, rows]
        )
        half_down(at).start()

    wg[c] = pltpu.roll(jnp.transpose(wy_ref[0]), 0, 1, stride=1, stride_axis=0)
    pl.semaphore_wait(
        barrier, n_z + 1 + has_above.astype(jnp.int32) + has_below.astype(jnp.int32)
    )
    to_x(z, x).start()
    to_core(z, x).start()
    for far in range(n_z - 1, -1, -1):
        @pl.when((far != z) & ((far < z) | (z < 2)))
        def _():
            to_z(far).start()

    @pl.when(jnp.logical_not(has_above))
    def _():
        above[...] = jnp.zeros_like(above)
        down_recv[...] = jnp.zeros_like(down_recv)

    @pl.when(jnp.logical_not(has_below))
    def _():
        up_recv[...] = jnp.zeros_like(up_recv)

    for i in range(chunks):
        xt[i] = jnp.transpose(eig_ref[i * band : (i + 1) * band, :])

    row = lax.broadcasted_iota(jnp.int32, (band, band), 0)
    col = lax.broadcasted_iota(jnp.int32, (band, band), 1)
    upper = col >= row
    zero = jnp.zeros((band, band), F32)

    def spread(w):
        return jnp.concatenate([jnp.where(upper, w, zero), jnp.where(upper, zero, w)], axis=1)

    def chosen(level, h):
        first = slot_ref[0, h, level] == 0
        return jnp.where(first, wg[level * per_level], wg[level * per_level + 1])

    def prepare(sheared, places):
        v_parts = [split(spread(w)) for w in sheared]
        grams = [product(v, v, NT) for v in v_parts]
        factors = inverses(grams, fast)
        for place, v, t in zip(places, v_parts, factors):
            z_parts = split(product(split(t), v))
            ops[place, 0] = z_parts[0]
            ops[place, 1] = z_parts[1]
            ops[place, 2] = v[0]
            ops[place, 3] = v[1]

    def reflected(places, pairs):
        halves = [split(pair) for pair in pairs]
        projected = [
            split(product(x, (ops[p, 0], ops[p, 1]), NT)) for p, x in zip(places, halves)
        ]
        return [
            pair - product(y, (ops[p, 2], ops[p, 3]))
            for p, y, pair in zip(places, projected, pairs)
        ]

    def window(top, bottom):
        return jnp.concatenate([top, bottom], axis=1)

    relay_z(0)

    @pl.when(z >= 2)
    def _():
        for far in range(n_z - 1, 2, -1):
            @pl.when(far > z)
            def _():
                to_z(far).start()

    relay_x(0)
    wait_core(0)

    @pl.when(has_below)
    def _():
        send_half(0)

    relay_z(1)
    prepare([chosen(0, 0), chosen(0, 1)], [3, 4])

    def both_levels(at, carry):
        @pl.when(has_above)
        def _():
            half_down(at).wait_recv()
            half_side(at).start()

        upper_new, lower_new = reflected([3, 4], [window(xt[0], xt[1]), window(xt[2], xt[3])])
        xt[0], xt[1] = upper_new[:, :band], upper_new[:, band:]
        xt[2], xt[3] = lower_new[:, :band], lower_new[:, band:]

        @pl.when(has_above)
        def _():
            up_send[at] = xt[0]
            go_up(at).start()

        @pl.when(has_below)
        def _():
            down_send[at] = xt[chunks - 1]
            go_down(at).start()

        @pl.when(at < rounds - 1)
        def _():
            relay_x(at + 1)
            wait_core(at + 1)

            @pl.when(has_below)
            def _():
                send_half(at + 1)

        @pl.when(at < rounds - 2)
        def _():
            relay_z(at + 2)

        @pl.when(has_above)
        def _():
            half_side(at).wait_recv()

        odd, even = 2 * at + 1, (2 * at + 2) % levels
        prepare(
            [chosen(odd, 0), chosen(odd, 1), above[at], chosen(even, 0), chosen(even, 1)],
            [0, 1, 2, 3, 4],
        )

        @pl.when(has_below)
        def _():
            go_up(at).wait_recv()

        @pl.when(has_above)
        def _():
            go_down(at).wait_recv()

        middle, last, first = reflected(
            [0, 1, 2],
            [
                window(xt[1], xt[2]),
                window(xt[chunks - 1], up_recv[at]),
                window(down_recv[at], xt[0]),
            ],
        )
        xt[1], xt[2] = middle[:, :band], middle[:, band:]
        xt[chunks - 1] = last[:, :band]
        xt[0] = jnp.where(has_above, first[:, band:], xt[0])
        return carry

    lax.fori_loop(0, rounds, both_levels, 0)

    for i in range(chunks):
        out_ref[i * band : (i + 1) * band, :] = jnp.transpose(xt[i])

    for zz in range(n_z):
        @pl.when(z != zz)
        def _():
            to_z(zz).wait_send()

    for zz in range(n_z):
        to_x(zz, x).wait_send()
        for xx in range(2):
            to_core(zz, xx).wait_send()
    for at in range(rounds):
        @pl.when(has_above)
        def _():
            go_up(at).wait_send()
            half_side(at).wait_send()

        @pl.when(has_below)
        def _():
            go_down(at).wait_send()
            half_down(at).wait_send()


def per_device(n_rows, n_cols, eigvecs, wy_packed, slot_block):
    band = wy_packed.shape[1]
    rows, cols = eigvecs.shape
    levels, per_level = slot_block.shape[1:]
    n_z = n_cols // 4
    rounds = levels // 2
    assert n_cols == levels * per_level and n_z == rounds
    assert wy_packed.shape[0] == 1 and per_level == 2 and rows == 4 * band
    blocks = pltpu.VMEM((rounds, band, band), F32)
    slots = pltpu.VMEM((rounds, cols, band), F32)
    vmem = pl.BlockSpec(memory_space=pltpu.VMEM)
    in_order = pltpu.SemaphoreType.DMA((2, rounds))
    return pl.pallas_call(
        functools.partial(kernel, levels, n_rows, n_z),
        out_shape=jax.ShapeDtypeStruct(eigvecs.shape, F32),
        in_specs=[pl.BlockSpec(memory_space=pltpu.SMEM), vmem, vmem],
        out_specs=vmem,
        scratch_shapes=[
            pltpu.VMEM((n_cols, band, band), F32),
            pltpu.VMEM((rows // band, cols, band), F32),
            pltpu.VMEM((5, 4, band, 2 * band), BF16),
            pltpu.VMEM((rounds, band // 2, band), F32),
            blocks,
            slots,
            slots,
            slots,
            slots,
            pltpu.SemaphoreType.DMA((n_cols,)),
            pltpu.SemaphoreType.DMA((n_cols // 2, 2)),
            pltpu.SemaphoreType.DMA((n_z,)),
            in_order,
            in_order,
            in_order,
            in_order,
        ],
        compiler_params=pltpu.CompilerParams(collective_id=0, has_side_effects=True),
    )(jnp.swapaxes(slot_block, 1, 2), eigvecs, wy_packed)


def solution(mesh):
    placed = (P("rows", "cols"), P(("rows", "cols"), None, None), P("rows", None, None))
    return jax.shard_map(
        functools.partial(per_device, mesh.shape["rows"], mesh.shape["cols"]),
        mesh=mesh, in_specs=placed, out_specs=P("rows", "cols"), check_vma=False,
    )
```
